32 devices in a mesh: band: 8 (over z, y), mode: 4 (over x, core).
Axes of the slice: x: 2, y: 2, z: 4, core: 2. Of those that a mesh axis runs over, the one named last changes fastest.
Arguments:
- velocity: bfloat16 [1, 8192, 1024], P(None, ('band', 'mode')), may hold values from -6 to 6
- radiation_modes: bfloat16 [8192, 1024], P('band', 'mode'), may hold values from -0.125 to 0.125
- resistance: float32 [8, 1024, 1024], P('band', None, 'mode'), as said below
- mode_ranks: int32 [8], P('band'), may hold values from 128 to 1024, as said below
- freq_table: int32 [512], replicated, may hold values from 0 to 511, each once
Outputs:
- adjoint_force: bfloat16 [1, 8192, 1024], P(None, ('band', 'mode'))
The draws below stay inside these ranges and needn't reach their ends.
Inputs may be any that keep to these rules, and one draw needn't show every extreme that they name: `resistance`: each band's matrix is symmetric. `mode_ranks`: the ranks never fall with the band index; the first band keeps 1024 // 8 modes and the last 1024.
All inputs are finite; a program needn't handle non-finite values.
Results may differ from the reference program's by a relative error of at most 0.015.
Values may be sent and summed in bfloat16 or wider, within the bound.
A program may use at most 64 MiB of HBM per device.

```python
import math
import jax
import jax.numpy as jnp
from jax import lax

WIN = 1
NT = 1024
F = 512
RMAX = 1024
PATCHES = 8192
NBANDS = 8
FPB = 64


def draw_resistance(key, part):
    first_key, second_key = jax.random.split(jax.random.fold_in(key, 11))
    noise = jax.random.normal(first_key, (NBANDS, RMAX, RMAX), jnp.float32)
    symmetric = (noise + jnp.swapaxes(noise, 1, 2)) * (0.5 / jnp.sqrt(jnp.float32(RMAX)))
    diagonal_part = jax.random.uniform(second_key, (NBANDS, RMAX), jnp.float32, 0.5, 2.0)
    identity = jnp.eye(RMAX, dtype=jnp.float32)
    return symmetric + diagonal_part[:, :, None] * identity[None, :, :]


def draw_mode_ranks(key, part):
    drawn = jax.random.randint(jax.random.fold_in(key, 23), (NBANDS,), RMAX // 8, RMAX + 1, jnp.int32)
    ordered = jnp.sort(drawn)
    ordered = ordered.at[0].set(RMAX // 8)
    ordered = ordered.at[NBANDS - 1].set(RMAX)
    return ordered.astype(jnp.int32)


def level_of(key, extent, cuts, least, top_value):
    def one(dim, parts):
        steps = jax.random.uniform(jax.random.fold_in(jax.random.fold_in(key, 6), dim), (parts,), jnp.float32, least / len(cuts), top_value / len(cuts))
        return jnp.repeat(jnp.exp(steps), extent[dim] // parts).reshape((-1,) + (1,) * (len(extent) - dim - 1))

    factor_of = one(*cuts[0])
    for cut in cuts[1:]:
        factor_of = factor_of * one(*cut)
    return factor_of


def normal_values(key, dims, scale, limit, cuts=(), kind=jnp.bfloat16):
    values = jax.random.normal(key, dims, jnp.float32) * scale
    if len(cuts) > 0:
        values = level_of(key, dims, cuts, -0.22, 0.18) * values
    return jnp.clip(values, min=-limit, max=limit).astype(kind)


def setup_inputs(seed: int = 0) -> dict:
    keys = jax.random.split(jax.random.key(seed), 6)
    velocity = normal_values(keys[0], (WIN, PATCHES, NT), 1.0, 6.0, ((1, 32),))
    radiation_modes = normal_values(keys[1], (PATCHES, RMAX), (PATCHES // 4) ** -0.5, 0.125, ((0, 8), (1, 4)))
    resistance = draw_resistance(jax.random.fold_in(keys[5], 71), 0)
    mode_ranks = draw_mode_ranks(jax.random.fold_in(keys[5], 71), 0)
    freq_table = jax.random.permutation(keys[4], F).astype(jnp.int32)
    return {"velocity": velocity, "radiation_modes": radiation_modes, "resistance": resistance, "mode_ranks": mode_ranks, "freq_table": freq_table}


def make_table(freq_table):
    times = jnp.arange(NT, dtype=jnp.int32)
    phases = times[:, None] * freq_table[None, :].astype(jnp.int32) % NT
    angles = phases.astype(jnp.float32) * (2.0 * math.pi / NT)
    norming = 1.0 / math.sqrt(NT)
    table = jnp.stack([jnp.cos(angles), -jnp.sin(angles)], axis=1) * norming
    return table.astype(jnp.bfloat16)

def reference(velocity, radiation_modes, resistance, mode_ranks, freq_table):
    table_wide = make_table(freq_table).astype(jnp.float32)
    modes_wide = radiation_modes.astype(jnp.float32)
    rank_mask = (jnp.arange(RMAX, dtype=jnp.int32)[:, None] < mode_ranks[None, :]).astype(jnp.float32)
    rank_mask = rank_mask[:, None, :, None]
    results = []
    for window in range(WIN):
        spectra = jnp.einsum('pt,tcf->pcf', velocity[window].astype(jnp.float32), table_wide).astype(jnp.bfloat16)
        coefficients = jnp.einsum('pr,pcf->rcf', modes_wide, spectra.astype(jnp.float32))
        coefficients = coefficients.reshape(RMAX, 2, NBANDS, FPB) * rank_mask
        forcing = jnp.einsum('bij,jcbf->icbf', resistance, coefficients, precision=lax.Precision.HIGHEST)
        forcing = (2.0 * forcing * rank_mask).astype(jnp.bfloat16).reshape(RMAX, 2, F)
        surface_force = jnp.einsum('pr,rcf->pcf', modes_wide, forcing.astype(jnp.float32)).astype(jnp.bfloat16)
        history = jnp.einsum('pcf,tcf->pt', surface_force.astype(jnp.float32), table_wide)
        results.append(history.astype(jnp.bfloat16))
    return jnp.stack(results, axis=0)
```

```python
import functools
import math

import jax
import jax.numpy as jnp
from jax import lax
from jax.experimental import pallas as pl
from jax.experimental.pallas import tpu as pltpu
from jax.sharding import PartitionSpec as P

MESH = pl.DeviceIdType.MESH
HALF_ROWS = 32


def cosine_of(phase, period):
    wrapped = phase & (period - 1)
    folded = jnp.minimum(wrapped, period - wrapped)
    flip = folded > period // 4
    folded = jnp.where(flip, period // 2 - folded, folded)
    x = folded.astype(jnp.float32) * (2.0 * math.pi / period)
    y = x * x
    value = jnp.full_like(y, 1.0 / math.factorial(16))
    for n in range(14, -1, -2):
        sign = -1.0 if n % 4 else 1.0
        value = value * y + sign / math.factorial(n)
    return jnp.where(flip, -value, value)


def ordered_offsets(n):
    offsets = [0]
    for step in range(1, n // 2 + 1):
        offsets.append(step)
        if n - step != step:
            offsets.append(n - step)
    return offsets[:n]


def fused_kernel(
    nb, nm, vel_ref, modes_ref, res_ref, rank_ref, freq_ref, out_ref,
    table, trig, modes_t, res_hi, res_lo, spec, part, rs, coef, force, basis, acc,
    bar_unused, sx_s, sx_r, sm_s, sm_r, sf_s, sf_r, rs_s, rs_r, k_s, k_r, ob_s, ob_r,
    f_s, f_r, fx_s, fx_r, fm_s, fm_r, ff_s, ff_r,
):
    b = lax.axis_index("band")
    m = lax.axis_index("mode")
    mate = m + 1 - 2 * (m % 2)
    cross = (m + 2) % nm
    diag = (mate + 2) % nm
    patches, steps = vel_ref.shape
    cols = table.shape[2]
    mode_cols = modes_ref.shape[1]

    def band_at(offset):
        return (b + offset) % nb

    def to_mode(src, dst, send, recv, target):
        return pltpu.make_async_remote_copy(
            src_ref=src, dst_ref=dst, send_sem=send, recv_sem=recv,
            device_id={"mode": target}, device_id_type=MESH)

    def to_band(src, dst, send, recv, target):
        return pltpu.make_async_remote_copy(
            src_ref=src, dst_ref=dst, send_sem=send, recv_sem=recv,
            device_id={"band": target}, device_id_type=MESH)

    barrier = pltpu.get_barrier_semaphore()
    for off in range(1, nm):
        pl.semaphore_signal(barrier, inc=1, device_id={"mode": (m + off) % nm}, device_id_type=MESH)
    for off in range(1, nb):
        pl.semaphore_signal(barrier, inc=1, device_id={"band": band_at(off)}, device_id_type=MESH)

    blocks = steps // HALF_ROWS
    norming = 1.0 / math.sqrt(steps)

    def build(k):
        freq = freq_ref[k]
        shift = freq_ref[nb]
        rows = lax.broadcasted_iota(jnp.int32, (HALF_ROWS, cols), 0)
        big = lax.broadcasted_iota(jnp.int32, (blocks, cols), 0) * HALF_ROWS
        low = rows * freq + shift
        high = big * freq
        quarter = steps // 4
        cos_low = cosine_of(low, steps) * norming
        sin_low = cosine_of(low - quarter, steps) * norming
        trig[0] = cosine_of(high, steps)
        trig[1] = cosine_of(high - quarter, steps)
        for a in range(blocks):
            row = trig[0, pl.ds(a, 1), :] * cos_low - trig[1, pl.ds(a, 1), :] * sin_low
            table[k, pl.ds(a * HALF_ROWS, HALF_ROWS), :] = row.astype(jnp.bfloat16)

    def spectra(k):
        build(k)
        spec[k, m] = jnp.dot(
            vel_ref[...], table[k], preferred_element_type=jnp.float32
        ).astype(jnp.bfloat16)

    order = [(i + 1) % nb for i in range(nb)]
    spectra(band_at(order[0]))
    pl.semaphore_wait(barrier, nm - 1 + nb - 1)

    def s_cross(k):
        return to_mode(spec.at[k, m], spec.at[k, m], sx_s.at[k], sx_r.at[k], cross)

    def s_mate(k):
        return to_mode(spec.at[k, m], spec.at[k, m], sm_s.at[k], sm_r.at[k], mate)

    def s_fwd(k):
        return to_mode(spec.at[k, cross], spec.at[k, cross], sf_s.at[k], sf_r.at[k], mate)

    def spec_step(i, _):
        k = (b + 1 + i) % nb
        s_cross(k).start()
        s_mate(k).start()

        nxt = (b + 2 + i) % nb
        spectra(nxt)
        return 0

    lax.fori_loop(0, nb - 1, spec_step, 0)
    s_cross(b).start()
    s_mate(b).start()

    def basis_copy(off):
        target = (m + off) % nm
        rows = pl.ds(pl.multiple_of(target * patches, patches), patches)
        return to_mode(modes_ref.at[rows], basis.at[m], ob_s.at[off], ob_r.at[off], target)

    for off in range(1, nm):
        basis_copy(off).start()
    modes_t[...] = modes_ref[...].T

    def partial(k):
        return jnp.dot(
            modes_t[...], spec[k].reshape(nm * patches, cols), preferred_element_type=jnp.float32)

    def rs_copy(k):
        return to_band(part.at[k], rs.at[b], rs_s.at[k], rs_r.at[b], k)

    def rs_arrival(k):
        return to_band(part.at[k], rs.at[k], rs_s.at[k], rs_r.at[k], k)

    def arrive(k):
        s_cross(k).wait_recv()
        s_fwd(k).start()

    def finish(k):
        s_mate(k).wait_recv()
        s_fwd(k).wait_recv()

    def part_step(i, _):
        k = (b + 1 + i) % nb
        arrive((b + 2 + i) % nb)
        finish(k)
        part[k] = partial(k).astype(jnp.bfloat16)
        rs_copy(k).start()
        return 0

    arrive(band_at(1))
    lax.fori_loop(0, nb - 1, part_step, 0)
    wide = res_ref[...].T
    narrow = wide.astype(jnp.bfloat16)
    res_hi[...] = narrow
    res_lo[...] = (wide - narrow.astype(jnp.float32)).astype(jnp.bfloat16)
    finish(b)
    total = partial(b)
    for off in range(1, nb):
        k = band_at(nb - off)
        rs_arrival(k).wait_recv()
        total = total + rs[k].astype(jnp.float32)
    kept = lax.broadcasted_iota(jnp.int32, (mode_cols, cols), 0) + m * mode_cols < rank_ref[0]
    total = jnp.where(kept, total, 0.0)
    coef[m] = total.astype(jnp.bfloat16)

    def k_copy(off):
        return to_mode(coef.at[m], coef.at[m], k_s.at[off], k_r.at[off], (m + off) % nm)

    def k_arrival(off):
        source = (m + nm - off) % nm
        return to_mode(coef.at[source], coef.at[source], k_s.at[off], k_r.at[off], source)

    for off in range(1, nm):
        k_copy(off).start()
    for off in range(1, nm):
        k_arrival(off).wait_recv()
    coefs = coef[...].reshape(nm * mode_cols, cols)
    forcing = jnp.dot(res_hi[...], coefs, preferred_element_type=jnp.float32) + jnp.dot(
        res_lo[...], coefs, preferred_element_type=jnp.float32)
    forcing = jnp.where(kept, 2.0 * forcing, 0.0)
    force[b, m] = forcing.astype(jnp.bfloat16)

    def f_copy(k):
        return to_band(force.at[b, m], force.at[b, m], f_s.at[k], f_r.at[b], k)

    def f_arrival(k):
        return to_band(force.at[k, m], force.at[k, m], f_s.at[k], f_r.at[k], k)

    def f_cross(k):
        return to_mode(force.at[k, m], force.at[k, m], fx_s.at[k], fx_r.at[k], cross)

    def f_mate(k):
        return to_mode(force.at[k, m], force.at[k, m], fm_s.at[k], fm_r.at[k], mate)

    def f_fwd(k):
        return to_mode(force.at[k, cross], force.at[k, cross], ff_s.at[k], ff_r.at[k], mate)

    offsets = ordered_offsets(nb)
    for off in offsets[1:]:
        f_copy(band_at(off)).start()
    f_cross(b).start()
    f_mate(b).start()

    for off in range(1, nm):
        source = (m + nm - off) % nm
        to_mode(basis.at[source], basis.at[source], ob_s.at[off], ob_r.at[off], source).wait_recv()
    basis[m] = modes_ref[pl.ds(pl.multiple_of(m * patches, patches), patches), :]

    def surface(k):
        value = jnp.dot(basis[0], force[k, 0], preferred_element_type=jnp.float32)
        for j in range(1, nm):
            value = value + jnp.dot(basis[j], force[k, j], preferred_element_type=jnp.float32)
        return value.astype(jnp.bfloat16)

    def history(k):
        f_mate(k).wait_recv()
        f_fwd(k).wait_recv()
        return lax.dot_general(
            surface(k), table[k], (((1,), (1,)), ((), ())), preferred_element_type=jnp.float32)

    for i in range(nb + 2):
        if 1 <= i < nb:
            k = band_at(offsets[i])
            f_arrival(k).wait_recv()
            f_cross(k).start()
            f_mate(k).start()
        if 1 <= i <= nb:
            k = band_at(offsets[i - 1])
            f_cross(k).wait_recv()
            f_fwd(k).start()
        if i >= 2:
            k = band_at(offsets[i - 2])
            term = history(k)
            if i == 2:
                acc[...] = term
            elif i < nb + 1:
                acc[...] += term
            else:
                out_ref[...] = (acc[...] + term).astype(out_ref.dtype)

    def drain(k, _):
        for copy in (s_cross, s_mate, s_fwd, f_cross, f_mate, f_fwd):
            copy(k).wait_send()
        return 0

    lax.fori_loop(0, nb, drain, 0)
    for off in range(1, nb):
        k = band_at(off)
        rs_copy(k).wait_send()
        f_copy(k).wait_send()
    for off in range(1, nm):
        basis_copy(off).wait_send()
        k_copy(off).wait_send()


def fused(mesh, velocity, radiation_modes, resistance, mode_ranks, freq_table):
    nb, nm = mesh.shape["band"], mesh.shape["mode"]
    patches, steps = velocity.shape[1:]
    mode_cols = radiation_modes.shape[1]
    modes = nm * mode_cols
    slots = freq_table.shape[0] // nb
    cols = 2 * slots
    by_band = freq_table.reshape(nb, 1, slots)
    freq_cols = jnp.concatenate([by_band, by_band], axis=2)
    shift = jnp.where(jnp.arange(cols, dtype=jnp.int32) < slots, 0, steps // 4)
    freq_cols = jnp.concatenate([freq_cols, shift.reshape(1, 1, cols).astype(jnp.int32)], axis=0)
    bf16, f32 = jnp.bfloat16, jnp.float32
    dma = lambda n: pltpu.SemaphoreType.DMA((n,))
    vmem = pl.BlockSpec(memory_space=pltpu.VMEM)
    out = pl.pallas_call(
        functools.partial(fused_kernel, nb, nm),
        out_shape=jax.ShapeDtypeStruct((patches, steps), bf16),
        in_specs=[vmem, vmem, vmem, pl.BlockSpec(memory_space=pltpu.SMEM), vmem],
        out_specs=vmem,
        scratch_shapes=[
            pltpu.VMEM((nb, steps, cols), bf16),
            pltpu.VMEM((2, steps // HALF_ROWS, cols), f32),
            pltpu.VMEM((mode_cols, nm * patches), bf16),
            pltpu.VMEM((mode_cols, modes), bf16),
            pltpu.VMEM((mode_cols, modes), bf16),
            pltpu.VMEM((nb, nm, patches, cols), bf16),
            pltpu.VMEM((nb, mode_cols, cols), bf16),
            pltpu.VMEM((nb, mode_cols, cols), bf16),
            pltpu.VMEM((nm, mode_cols, cols), bf16),
            pltpu.VMEM((nb, nm, mode_cols, cols), bf16),
            pltpu.VMEM((nm, patches, mode_cols), bf16),
            pltpu.VMEM((patches, steps), f32),
            pltpu.SemaphoreType.REGULAR,
        ]
        + [dma(nb) for _ in range(8)]
        + [dma(nm) for _ in range(4)]
        + [dma(nb) for _ in range(8)],
        compiler_params=pltpu.CompilerParams(collective_id=0, has_side_effects=True),
    )(velocity[0], radiation_modes, resistance[0], mode_ranks, freq_cols)
    return out[None]


def make_table(freq_table, step_count):
    times = jnp.arange(step_count, dtype=jnp.int32)
    phases = times[:, None] * freq_table[None, :] % step_count
    angles = phases.astype(jnp.float32) * (2.0 * math.pi / step_count)
    norming = 1.0 / math.sqrt(step_count)
    table = jnp.stack([jnp.cos(angles), -jnp.sin(angles)], axis=1) * norming
    return table.astype(jnp.bfloat16)


def add_sources(received):
    return jnp.sum(received, axis=0)


def per_device(velocity, radiation_modes, resistance, mode_ranks, freq_table):
    step_count = velocity.shape[2]
    mode_cols = radiation_modes.shape[1]
    dft_table = make_table(freq_table, step_count)
    spectra = jnp.einsum(
        "wpt,tcf->wpcf", velocity, dft_table, preferred_element_type=jnp.float32
    ).astype(jnp.bfloat16)
    partial_value = jnp.einsum(
        "wpcf,pr->wrcf",
        lax.all_gather(spectra, "mode", axis=1, tiled=True),
        radiation_modes,
        preferred_element_type=jnp.float32,
    )
    coefficients = add_sources(
        lax.all_to_all(
            partial_value[None].astype(jnp.bfloat16),
            "band",
            split_axis=4,
            concat_axis=0,
            tiled=True,
        ).astype(jnp.float32)
    )
    offset = lax.axis_index("mode") * mode_cols
    rank_here = mode_ranks[0]
    kept_mask = (offset + jnp.arange(mode_cols, dtype=jnp.int32) < rank_here).astype(jnp.float32)
    kept_mask = kept_mask[None, :, None, None]
    coefficients = coefficients * kept_mask
    matrix = resistance[0]
    partial_terms = jnp.einsum(
        "ij,wjcf->wicf", matrix, coefficients, precision=lax.Precision.HIGHEST
    )
    forcing = lax.psum_scatter(
        partial_terms.astype(jnp.bfloat16), "mode", scatter_dimension=1, tiled=True
    ).astype(jnp.float32)
    forcing = (2.0 * forcing * kept_mask).astype(jnp.bfloat16)
    collected = lax.all_gather(forcing, "mode", axis=1, tiled=True)
    collected = lax.all_gather(collected, "band", axis=3, tiled=True)
    own_basis = lax.all_to_all(radiation_modes, "mode", split_axis=0, concat_axis=1, tiled=True)
    surface_force = jnp.einsum(
        "pr,wrcf->wpcf", own_basis, collected, preferred_element_type=jnp.float32
    ).astype(jnp.bfloat16)
    history = jnp.einsum(
        "wpcf,tcf->wpt", surface_force, dft_table, preferred_element_type=jnp.float32
    )
    return history.astype(jnp.bfloat16)


def solution(mesh):
    placed = (
        P(None, ("band", "mode"), None),
        P("band", "mode"),
        P("band", None, "mode"),
        P("band"),
        P(),
    )
    nb, nm = mesh.shape["band"], mesh.shape["mode"]

    def body(velocity, radiation_modes, resistance, mode_ranks, freq_table):
        windows, patches, steps = velocity.shape
        mode_cols = radiation_modes.shape[1]
        cols = 2 * (freq_table.shape[0] // nb)
        tiled = (
            windows == 1 and nm == 4 and nb > 1 and cols % 128 == 0 and mode_cols % 128 == 0
            and patches % 128 == 0 and steps % 128 == 0 and steps & (steps - 1) == 0
        )
        args = (velocity, radiation_modes, resistance, mode_ranks, freq_table)
        return fused(mesh, *args) if tiled else per_device(*args)

    return jax.shard_map(
        body,
        mesh=mesh,
        in_specs=placed,
        out_specs=P(None, ("band", "mode"), None),
        check_vma=False,
    )
```

```python
import functools
import math

import jax
import jax.numpy as jnp
from jax import lax
from jax.experimental import pallas as pl
from jax.experimental.pallas import tpu as pltpu
from jax.sharding import PartitionSpec as P

MESH = pl.DeviceIdType.MESH
HALF_ROWS = 32


def cosine_of(phase, period):
    wrapped = phase & (period - 1)
    folded = jnp.minimum(wrapped, period - wrapped)
    flip = folded > period // 4
    folded = jnp.where(flip, period // 2 - folded, folded)
    x = folded.astype(jnp.float32) * (2.0 * math.pi / period)
    y = x * x
    value = jnp.full_like(y, 1.0 / math.factorial(16))
    for n in range(14, -1, -2):
        sign = -1.0 if n % 4 else 1.0
        value = value * y + sign / math.factorial(n)
    return jnp.where(flip, -value, value)


def fused_kernel(
    nb, nm, vel_ref, modes_ref, res_ref, rank_ref, freq_ref, out_ref,
    table, trig, modes_t, res_hi, res_lo, spec, part, pair, rs, coef, force, basis, acc,
    sx_s, sx_r, sm_s, sm_r, sf_s, sf_r, rs_s, rs_r, ry_s, ry_r, k_s, k_r, ob_s, ob_r,
    fz_s, fz_r, fy_s, fy_r, fx_s, fx_r, gy_s, gy_r, gx_s, gx_r, fm_s, fm_r, ff_s, ff_r,
):
    b = lax.axis_index("band")
    m = lax.axis_index("mode")
    mate = m + 1 - 2 * (m % 2)
    cross = (m + 2) % nm
    diag = (mate + 2) % nm
    patches, steps = vel_ref.shape
    cols = table.shape[2]
    mode_cols = modes_ref.shape[1]

    def band_at(e):
        bits = [1 << i for i in range(nb.bit_length() - 1)]
        return sum(bit * ((b // bit + e // bit) % 2) for bit in bits)

    def to_mode(src, dst, send, recv, target):
        return pltpu.make_async_remote_copy(
            src_ref=src, dst_ref=dst, send_sem=send, recv_sem=recv,
            device_id={"mode": target}, device_id_type=MESH)

    def to_band(src, dst, send, recv, target):
        return pltpu.make_async_remote_copy(
            src_ref=src, dst_ref=dst, send_sem=send, recv_sem=recv,
            device_id={"band": target}, device_id_type=MESH)

    barrier = pltpu.get_barrier_semaphore()
    for off in range(1, nm):
        pl.semaphore_signal(barrier, inc=1, device_id={"mode": (m + off) % nm}, device_id_type=MESH)
    for off in range(1, nb):
        pl.semaphore_signal(barrier, inc=1, device_id={"band": band_at(off)}, device_id_type=MESH)

    blocks = steps // HALF_ROWS
    norming = 1.0 / math.sqrt(steps)

    def build(k):
        half = cols // 2
        lane = lax.broadcasted_iota(jnp.int32, (HALF_ROWS, cols), 1)
        row = jnp.broadcast_to(freq_ref[pl.ds(k // 2, 1), :], (HALF_ROWS, cols))
        freq = jnp.where(lane // half == k % 2, row, pltpu.roll(row, half, 1))
        shift = jnp.where(lane < half, 0, steps // 4)
        rows = lax.broadcasted_iota(jnp.int32, (HALF_ROWS, cols), 0)
        big = lax.broadcasted_iota(jnp.int32, (blocks, cols), 0) * HALF_ROWS
        low = rows * freq + shift
        high = big * freq
        quarter = steps // 4
        cos_low = cosine_of(low, steps) * norming
        sin_low = cosine_of(low - quarter, steps) * norming
        trig[0] = cosine_of(high, steps)
        trig[1] = cosine_of(high - quarter, steps)
        for a in range(blocks):
            row = trig[0, pl.ds(a, 1), :] * cos_low - trig[1, pl.ds(a, 1), :] * sin_low
            table[k, pl.ds(a * HALF_ROWS, HALF_ROWS), :] = row.astype(jnp.bfloat16)

    def spectra(k):
        build(k)
        spec[k, m] = jnp.dot(
            vel_ref[...], table[k], preferred_element_type=jnp.float32
        ).astype(jnp.bfloat16)

    spectra(band_at(nb - 1))
    pl.semaphore_wait(barrier, nm - 1 + nb - 1)

    def s_cross(k):
        return to_mode(spec.at[k, m], spec.at[k, m], sx_s.at[k], sx_r.at[k], cross)

    def s_mate(k):
        return to_mode(spec.at[k, m], spec.at[k, m], sm_s.at[k], sm_r.at[k], mate)

    def s_fwd(k):
        return to_mode(spec.at[k, cross], spec.at[k, cross], sf_s.at[k], sf_r.at[k], mate)

    def spec_step(i, _):
        k = band_at(nb - 1 - i)
        s_cross(k).start()
        s_mate(k).start()
        spectra(band_at(nb - 2 - i))
        return 0

    lax.fori_loop(0, nb - 1, spec_step, 0)
    s_cross(b).start()
    s_mate(b).start()

    near = band_at(1)

    def basis_copy(off):
        target = (m + off) % nm
        rows = pl.ds(pl.multiple_of(target * patches, patches), patches)
        return to_mode(modes_ref.at[rows], basis.at[m], ob_s.at[off], ob_r.at[off], target)

    for off in range(1, nm):
        basis_copy(off).start()
    modes_t[...] = modes_ref[...].T
    wide = res_ref[...].T
    narrow = wide.astype(jnp.bfloat16)
    res_hi[...] = narrow
    res_lo[...] = (wide - narrow.astype(jnp.float32)).astype(jnp.bfloat16)

    def partial(k):
        return jnp.dot(
            modes_t[...], spec[k].reshape(nm * patches, cols), preferred_element_type=jnp.float32)

    def rs_copy(k):
        return to_band(part.at[k], rs.at[b], rs_s.at[k], rs_r.at[b], k)

    def rs_arrival(k):
        return to_band(part.at[k], rs.at[k], rs_s.at[k], rs_r.at[k], k)

    def arrive(k):
        s_cross(k).wait_recv()
        s_fwd(k).start()

    def finish(k):
        s_mate(k).wait_recv()
        s_fwd(k).wait_recv()

    def pair_copy(k):
        return to_band(part.at[k], pair.at[k], ry_s.at[k], ry_r.at[k], near)

    def with_pair(k):
        value = partial(k)
        pair_copy(k).wait_recv()
        return value + pair[k].astype(jnp.float32)

    def part_step(i, _):
        e = nb - 1 - 2 * i
        other, mine = band_at(e), band_at(e - 1)
        arrive(mine)
        finish(other)
        part[other] = partial(other).astype(jnp.bfloat16)
        pair_copy(other).start()
        arrive(band_at(e - 2))
        finish(mine)
        part[mine] = with_pair(mine).astype(jnp.bfloat16)
        rs_copy(mine).start()
        return 0

    arrive(band_at(nb - 1))
    lax.fori_loop(0, nb // 2 - 1, part_step, 0)
    arrive(b)
    finish(near)
    part[near] = partial(near).astype(jnp.bfloat16)
    pair_copy(near).start()
    finish(b)
    total = with_pair(b)
    for e in range(nb - 2, 0, -2):
        k = band_at(e)
        rs_arrival(k).wait_recv()
        total = total + rs[k].astype(jnp.float32)
    kept = lax.broadcasted_iota(jnp.int32, (mode_cols, cols), 0) + m * mode_cols < rank_ref[...]
    total = jnp.where(kept, total, 0.0)
    coef[m] = total.astype(jnp.bfloat16)

    k_copies = [
        to_mode(coef.at[slot], coef.at[slot], k_s.at[i], k_r.at[i], target)
        for i, (slot, target) in enumerate([(m, cross), (m, mate), (cross, mate)])
    ]
    k_copies[0].start()
    k_copies[1].start()
    k_copies[0].wait_recv()
    k_copies[2].start()
    k_copies[1].wait_recv()
    k_copies[2].wait_recv()
    coefs = coef[...].reshape(nm * mode_cols, cols)
    forcing = jnp.dot(res_hi[...], coefs, preferred_element_type=jnp.float32) + jnp.dot(
        res_lo[...], coefs, preferred_element_type=jnp.float32)
    forcing = jnp.where(kept, 2.0 * forcing, 0.0)
    force[b, m] = forcing.astype(jnp.bfloat16)

    half = mode_cols // 2
    upper, lower = pl.ds(0, half), pl.ds(half, half)

    def f_far(k):
        return to_band(force.at[b, m], force.at[b, m], fz_s.at[k], fz_r.at[b], k)

    def f_far_arrival(k):
        return to_band(force.at[k, m], force.at[k, m], fz_s.at[k], fz_r.at[k], k)

    def f_near(k):
        return to_band(force.at[k, m], force.at[k, m], fy_s.at[k], fy_r.at[k], near)

    def f_cross(k):
        return to_mode(force.at[k, m], force.at[k, m], fx_s.at[k], fx_r.at[k], cross)

    def g_near(k):
        piece = force.at[k, cross, lower]
        return to_band(piece, piece, gy_s.at[k], gy_r.at[k], near)

    def g_cross(k):
        piece = force.at[k, m, upper]
        return to_mode(piece, piece, gx_s.at[k], gx_r.at[k], cross)

    def f_mate(k):
        return to_mode(force.at[k, m], force.at[k, m], fm_s.at[k], fm_r.at[k], mate)

    def f_fwd(k):
        return to_mode(force.at[k, cross], force.at[k, cross], ff_s.at[k], ff_r.at[k], mate)

    far = list(range(0, nb, 2))

    def first(j):
        k = band_at(far[j])
        if j > 0:
            f_far_arrival(k).wait_recv()
        f_near(k).start()
        f_cross(k).start()
        f_mate(k).start()

    def second(j):
        k, k1 = band_at(far[j]), band_at(far[j] + 1)
        f_near(k1).wait_recv()
        g_cross(k1).start()
        f_mate(k1).start()
        f_cross(k).wait_recv()
        g_near(k).start()
        f_fwd(k).start()

    def third(j):
        k1 = band_at(far[j] + 1)
        g_cross(k1).wait_recv()
        g_near(k1).wait_recv()
        f_fwd(k1).start()

    for e in far[1:]:
        f_far(band_at(e)).start()
    first(0)

    for off in range(1, nm):
        source = (m + nm - off) % nm
        to_mode(basis.at[source], basis.at[source], ob_s.at[off], ob_r.at[off], source).wait_recv()
    basis[m] = modes_ref[pl.ds(pl.multiple_of(m * patches, patches), patches), :]

    def surface(k):
        value = jnp.dot(basis[0], force[k, 0], preferred_element_type=jnp.float32)
        for j in range(1, nm):
            value = value + jnp.dot(basis[j], force[k, j], preferred_element_type=jnp.float32)
        return value.astype(jnp.bfloat16)

    def history(k):
        f_mate(k).wait_recv()
        f_fwd(k).wait_recv()
        return lax.dot_general(
            surface(k), table[k], (((1,), (1,)), ((), ())), preferred_element_type=jnp.float32)

    def last(e):
        term = history(band_at(e))
        if e == 0:
            acc[...] = term
        elif e < nb - 1:
            acc[...] += term
        else:
            out_ref[...] = (acc[...] + term).astype(out_ref.dtype)

    n = len(far)
    for j in range(1, n):
        first(j)
    for j in range(n):
        second(j)
    for j in range(n - 1):
        last(far[j])
        third(j)
    third(n - 1)
    last(far[n - 1])
    for j in range(n):
        last(far[j] + 1)

    def drain(k, _):
        for copy in (s_cross, s_mate, s_fwd, f_mate, f_fwd):
            copy(k).wait_send()
        return 0

    lax.fori_loop(0, nb, drain, 0)
    for e in far:
        k, k1 = band_at(e), band_at(e + 1)
        pair_copy(k1).wait_send()
        if e > 0:
            f_far(k).wait_send()
            rs_copy(k).wait_send()
        f_near(k).wait_send()
        f_cross(k).wait_send()
        g_near(k).wait_send()
        g_cross(k1).wait_send()
    for off in range(1, nm):
        basis_copy(off).wait_send()
    for copy in k_copies:
        copy.wait_send()


def fused(mesh, velocity, radiation_modes, resistance, mode_ranks, freq_table):
    nb, nm = mesh.shape["band"], mesh.shape["mode"]
    patches, steps = velocity.shape[1:]
    mode_cols = radiation_modes.shape[1]
    modes = nm * mode_cols
    cols = 2 * (freq_table.shape[0] // nb)
    bf16, f32 = jnp.bfloat16, jnp.float32
    dma = lambda n: pltpu.SemaphoreType.DMA((n,))
    vmem = pl.BlockSpec(memory_space=pltpu.VMEM)
    out = pl.pallas_call(
        functools.partial(fused_kernel, nb, nm),
        out_shape=jax.ShapeDtypeStruct((patches, steps), bf16),
        in_specs=[vmem] * 5,
        out_specs=vmem,
        scratch_shapes=[
            pltpu.VMEM((nb, steps, cols), bf16),
            pltpu.VMEM((2, steps // HALF_ROWS, cols), f32),
            pltpu.VMEM((mode_cols, nm * patches), bf16),
            pltpu.VMEM((mode_cols, modes), bf16),
            pltpu.VMEM((mode_cols, modes), bf16),
            pltpu.VMEM((nb, nm, patches, cols), bf16),
            pltpu.VMEM((nb, mode_cols, cols), bf16),
            pltpu.VMEM((nb, mode_cols, cols), bf16),
            pltpu.VMEM((nb, mode_cols, cols), bf16),
            pltpu.VMEM((nm, mode_cols, cols), bf16),
            pltpu.VMEM((nb, nm, mode_cols, cols), bf16),
            pltpu.VMEM((nm, patches, mode_cols), bf16),
            pltpu.VMEM((patches, steps), f32),
            ]
        + [dma(nb) for _ in range(10)]
        + [dma(nm) for _ in range(4)]
        + [dma(nb) for _ in range(14)],
        compiler_params=pltpu.CompilerParams(collective_id=0, has_side_effects=True),
    )(velocity[0], radiation_modes, resistance[0], mode_ranks.reshape(1, 1), freq_table.reshape(nb // 2, cols))
    return out[None]


def make_table(freq_table, step_count):
    times = jnp.arange(step_count, dtype=jnp.int32)
    phases = times[:, None] * freq_table[None, :] % step_count
    angles = phases.astype(jnp.float32) * (2.0 * math.pi / step_count)
    norming = 1.0 / math.sqrt(step_count)
    table = jnp.stack([jnp.cos(angles), -jnp.sin(angles)], axis=1) * norming
    return table.astype(jnp.bfloat16)


def add_sources(received):
    return jnp.sum(received, axis=0)


def per_device(velocity, radiation_modes, resistance, mode_ranks, freq_table):
    step_count = velocity.shape[2]
    mode_cols = radiation_modes.shape[1]
    dft_table = make_table(freq_table, step_count)
    spectra = jnp.einsum(
        "wpt,tcf->wpcf", velocity, dft_table, preferred_element_type=jnp.float32
    ).astype(jnp.bfloat16)
    partial_value = jnp.einsum(
        "wpcf,pr->wrcf",
        lax.all_gather(spectra, "mode", axis=1, tiled=True),
        radiation_modes,
        preferred_element_type=jnp.float32,
    )
    coefficients = add_sources(
        lax.all_to_all(
            partial_value[None].astype(jnp.bfloat16),
            "band",
            split_axis=4,
            concat_axis=0,
            tiled=True,
        ).astype(jnp.float32)
    )
    offset = lax.axis_index("mode") * mode_cols
    rank_here = mode_ranks[0]
    kept_mask = (offset + jnp.arange(mode_cols, dtype=jnp.int32) < rank_here).astype(jnp.float32)
    kept_mask = kept_mask[None, :, None, None]
    coefficients = coefficients * kept_mask
    matrix = resistance[0]
    partial_terms = jnp.einsum(
        "ij,wjcf->wicf", matrix, coefficients, precision=lax.Precision.HIGHEST
    )
    forcing = lax.psum_scatter(
        partial_terms.astype(jnp.bfloat16), "mode", scatter_dimension=1, tiled=True
    ).astype(jnp.float32)
    forcing = (2.0 * forcing * kept_mask).astype(jnp.bfloat16)
    collected = lax.all_gather(forcing, "mode", axis=1, tiled=True)
    collected = lax.all_gather(collected, "band", axis=3, tiled=True)
    own_basis = lax.all_to_all(radiation_modes, "mode", split_axis=0, concat_axis=1, tiled=True)
    surface_force = jnp.einsum(
        "pr,wrcf->wpcf", own_basis, collected, preferred_element_type=jnp.float32
    ).astype(jnp.bfloat16)
    history = jnp.einsum(
        "wpcf,tcf->wpt", surface_force, dft_table, preferred_element_type=jnp.float32
    )
    return history.astype(jnp.bfloat16)


def solution(mesh):
    placed = (
        P(None, ("band", "mode"), None),
        P("band", "mode"),
        P("band", None, "mode"),
        P("band"),
        P(),
    )
    nb, nm = mesh.shape["band"], mesh.shape["mode"]

    def body(velocity, radiation_modes, resistance, mode_ranks, freq_table):
        windows, patches, steps = velocity.shape
        mode_cols = radiation_modes.shape[1]
        cols = 2 * (freq_table.shape[0] // nb)
        tiled = (
            windows == 1 and nm == 4 and nb > 2 and nb & (nb - 1) == 0 and cols == 128 and mode_cols % 128 == 0
            and patches % 128 == 0 and steps % 128 == 0 and steps & (steps - 1) == 0
        )
        args = (velocity, radiation_modes, resistance, mode_ranks, freq_table)
        return fused(mesh, *args) if tiled else per_device(*args)

    return jax.shard_map(
        body,
        mesh=mesh,
        in_specs=placed,
        out_specs=P(None, ("band", "mode"), None),
        check_vma=False,
    )
```

```python
import functools
import math

import jax
import jax.numpy as jnp
from jax import lax
from jax.experimental import pallas as pl
from jax.experimental.pallas import tpu as pltpu
from jax.sharding import PartitionSpec as P

MESH = pl.DeviceIdType.MESH
HALF_ROWS = 32


def cosine_of(phase, period):
    wrapped = phase & (period - 1)
    folded = jnp.minimum(wrapped, period - wrapped)
    flip = folded > period // 4
    folded = jnp.where(flip, period // 2 - folded, folded)
    x = folded.astype(jnp.float32) * (2.0 * math.pi / period)
    y = x * x
    value = jnp.full_like(y, 1.0 / math.factorial(16))
    for n in range(14, -1, -2):
        sign = -1.0 if n % 4 else 1.0
        value = value * y + sign / math.factorial(n)
    return jnp.where(flip, -value, value)


def fused_kernel(
    nb, nm, vel_ref, modes_ref, res_ref, rank_ref, freq_ref, out_ref,
    table, trig, modes_t, res_hi, res_lo, spec, part, rs, coef, force, basis, acc,
    sx_s, sx_r, sm_s, sm_r, sf_s, sf_r, rs_s, rs_r, k_s, k_r, ob_s, ob_r,
    fz_s, fz_r, fy_s, fy_r, fx_s, fx_r, gy_s, gy_r, gx_s, gx_r, fm_s, fm_r, ff_s, ff_r,
):
    b = lax.axis_index("band")
    m = lax.axis_index("mode")
    mate = m + 1 - 2 * (m % 2)
    cross = (m + 2) % nm
    diag = (mate + 2) % nm
    patches, steps = vel_ref.shape
    cols = table.shape[2]
    mode_cols = modes_ref.shape[1]

    def band_at(e):
        bits = [1 << i for i in range(nb.bit_length() - 1)]
        return sum(bit * ((b // bit + e // bit) % 2) for bit in bits)

    def to_mode(src, dst, send, recv, target):
        return pltpu.make_async_remote_copy(
            src_ref=src, dst_ref=dst, send_sem=send, recv_sem=recv,
            device_id={"mode": target}, device_id_type=MESH)

    def to_band(src, dst, send, recv, target):
        return pltpu.make_async_remote_copy(
            src_ref=src, dst_ref=dst, send_sem=send, recv_sem=recv,
            device_id={"band": target}, device_id_type=MESH)

    barrier = pltpu.get_barrier_semaphore()
    for off in range(1, nm):
        pl.semaphore_signal(barrier, inc=1, device_id={"mode": (m + off) % nm}, device_id_type=MESH)
    for off in range(1, nb):
        pl.semaphore_signal(barrier, inc=1, device_id={"band": band_at(off)}, device_id_type=MESH)

    blocks = steps // HALF_ROWS
    norming = 1.0 / math.sqrt(steps)

    def build(k):
        half = cols // 2
        lane = lax.broadcasted_iota(jnp.int32, (HALF_ROWS, cols), 1)
        row = jnp.broadcast_to(freq_ref[pl.ds(k // 2, 1), :], (HALF_ROWS, cols))
        freq = jnp.where(lane // half == k % 2, row, pltpu.roll(row, half, 1))
        shift = jnp.where(lane < half, 0, steps // 4)
        rows = lax.broadcasted_iota(jnp.int32, (HALF_ROWS, cols), 0)
        big = lax.broadcasted_iota(jnp.int32, (blocks, cols), 0) * HALF_ROWS
        low = rows * freq + shift
        high = big * freq
        quarter = steps // 4
        cos_low = cosine_of(low, steps) * norming
        sin_low = cosine_of(low - quarter, steps) * norming
        trig[0] = cosine_of(high, steps)
        trig[1] = cosine_of(high - quarter, steps)
        for a in range(blocks):
            row = trig[0, pl.ds(a, 1), :] * cos_low - trig[1, pl.ds(a, 1), :] * sin_low
            table[k, pl.ds(a * HALF_ROWS, HALF_ROWS), :] = row.astype(jnp.bfloat16)

    def spectra(k):
        build(k)
        spec[k, m] = jnp.dot(
            vel_ref[...], table[k], preferred_element_type=jnp.float32
        ).astype(jnp.bfloat16)

    spectra(band_at(nb - 1))
    modes_t[...] = modes_ref[...].T
    wide = res_ref[...].T
    narrow = wide.astype(jnp.bfloat16)
    res_hi[...] = narrow
    res_lo[...] = (wide - narrow.astype(jnp.float32)).astype(jnp.bfloat16)
    pl.semaphore_wait(barrier, nm - 1 + nb - 1)

    def s_cross(k):
        return to_mode(spec.at[k, m], spec.at[k, m], sx_s.at[k], sx_r.at[k], cross)

    def s_mate(k):
        return to_mode(spec.at[k, m], spec.at[k, m], sm_s.at[k], sm_r.at[k], mate)

    def s_fwd(k):
        return to_mode(spec.at[k, cross], spec.at[k, cross], sf_s.at[k], sf_r.at[k], mate)

    def spec_step(i, _):
        k = band_at(nb - 1 - i)
        s_cross(k).start()
        s_mate(k).start()
        spectra(band_at(nb - 2 - i))
        return 0

    lax.fori_loop(0, nb - 1, spec_step, 0)
    s_cross(b).start()
    s_mate(b).start()

    def basis_copy(off):
        target = (m + off) % nm
        rows = pl.ds(pl.multiple_of(target * patches, patches), patches)
        return to_mode(modes_ref.at[rows], basis.at[m], ob_s.at[off], ob_r.at[off], target)

    for off in range(1, nm):
        basis_copy(off).start()
    def partial(k):
        return jnp.dot(
            modes_t[...], spec[k].reshape(nm * patches, cols), preferred_element_type=jnp.float32)

    def rs_copy(k):
        return to_band(part.at[k], rs.at[b], rs_s.at[k], rs_r.at[b], k)

    def rs_arrival(k):
        return to_band(part.at[k], rs.at[k], rs_s.at[k], rs_r.at[k], k)

    def arrive(k):
        s_cross(k).wait_recv()
        s_fwd(k).start()

    def finish(k):
        s_mate(k).wait_recv()
        s_fwd(k).wait_recv()

    def part_step(i, _):
        k = band_at(nb - 1 - i)
        arrive(band_at(nb - 2 - i))
        finish(k)
        part[k] = partial(k).astype(jnp.bfloat16)
        rs_copy(k).start()
        return 0

    arrive(band_at(nb - 1))
    lax.fori_loop(0, nb - 1, part_step, 0)
    finish(b)
    total = partial(b)
    for off in range(1, nb):
        k = band_at(nb - off)
        rs_arrival(k).wait_recv()
        total = total + rs[k].astype(jnp.float32)
    kept = lax.broadcasted_iota(jnp.int32, (mode_cols, cols), 0) + m * mode_cols < rank_ref[...]
    total = jnp.where(kept, total, 0.0)
    coef[m] = total.astype(jnp.bfloat16)

    def k_copy(off):
        return to_mode(coef.at[m], coef.at[m], k_s.at[off], k_r.at[off], (m + off) % nm)

    def k_arrival(off):
        source = (m + nm - off) % nm
        return to_mode(coef.at[source], coef.at[source], k_s.at[off], k_r.at[off], source)

    for off in range(1, nm):
        k_copy(off).start()
    for off in range(1, nm):
        k_arrival(off).wait_recv()
    coefs = coef[...].reshape(nm * mode_cols, cols)
    forcing = jnp.dot(res_hi[...], coefs, preferred_element_type=jnp.float32) + jnp.dot(
        res_lo[...], coefs, preferred_element_type=jnp.float32)
    forcing = jnp.where(kept, 2.0 * forcing, 0.0)
    force[b, m] = forcing.astype(jnp.bfloat16)

    half = mode_cols // 2
    upper, lower = pl.ds(0, half), pl.ds(half, half)
    near = band_at(1)

    def f_far(k):
        return to_band(force.at[b, m], force.at[b, m], fz_s.at[k], fz_r.at[b], k)

    def f_far_arrival(k):
        return to_band(force.at[k, m], force.at[k, m], fz_s.at[k], fz_r.at[k], k)

    def f_near(k):
        return to_band(force.at[k, m], force.at[k, m], fy_s.at[k], fy_r.at[k], near)

    def f_cross(k):
        return to_mode(force.at[k, m], force.at[k, m], fx_s.at[k], fx_r.at[k], cross)

    def g_near(k):
        piece = force.at[k, cross, lower]
        return to_band(piece, piece, gy_s.at[k], gy_r.at[k], near)

    def g_cross(k):
        piece = force.at[k, m, upper]
        return to_mode(piece, piece, gx_s.at[k], gx_r.at[k], cross)

    def f_mate(k):
        return to_mode(force.at[k, m], force.at[k, m], fm_s.at[k], fm_r.at[k], mate)

    def f_fwd(k):
        return to_mode(force.at[k, cross], force.at[k, cross], ff_s.at[k], ff_r.at[k], mate)

    far = list(range(0, nb, 2))

    def first(j):
        k = band_at(far[j])
        if j > 0:
            f_far_arrival(k).wait_recv()
        f_near(k).start()
        f_cross(k).start()
        f_mate(k).start()

    def second(j):
        k, k1 = band_at(far[j]), band_at(far[j] + 1)
        f_near(k1).wait_recv()
        g_cross(k1).start()
        f_mate(k1).start()
        f_cross(k).wait_recv()
        g_near(k).start()
        f_fwd(k).start()

    def third(j):
        k1 = band_at(far[j] + 1)
        g_cross(k1).wait_recv()
        g_near(k1).wait_recv()
        f_fwd(k1).start()

    for e in far[1:]:
        f_far(band_at(e)).start()
    first(0)

    for off in range(1, nm):
        source = (m + nm - off) % nm
        to_mode(basis.at[source], basis.at[source], ob_s.at[off], ob_r.at[off], source).wait_recv()
    basis[m] = modes_ref[pl.ds(pl.multiple_of(m * patches, patches), patches), :]

    def surface(k):
        value = jnp.dot(basis[0], force[k, 0], preferred_element_type=jnp.float32)
        for j in range(1, nm):
            value = value + jnp.dot(basis[j], force[k, j], preferred_element_type=jnp.float32)
        return value.astype(jnp.bfloat16)

    def history(k):
        f_mate(k).wait_recv()
        f_fwd(k).wait_recv()
        return lax.dot_general(
            surface(k), table[k], (((1,), (1,)), ((), ())), preferred_element_type=jnp.float32)

    def last(e):
        term = history(band_at(e))
        if e == 0:
            acc[...] = term
        elif e < nb - 1:
            acc[...] += term
        else:
            out_ref[...] = (acc[...] + term).astype(out_ref.dtype)

    n = len(far)
    for j in range(1, n):
        first(j)
    for j in range(n):
        second(j)
    for j in range(n - 1):
        last(far[j])
        third(j)
    third(n - 1)
    last(far[n - 1])
    for j in range(n):
        last(far[j] + 1)

    def drain(k, _):
        for copy in (s_cross, s_mate, s_fwd, f_mate, f_fwd):
            copy(k).wait_send()
        return 0

    lax.fori_loop(0, nb, drain, 0)
    for off in range(1, nb):
        k = band_at(off)
        rs_copy(k).wait_send()
    for e in far:
        k, k1 = band_at(e), band_at(e + 1)
        if e > 0:
            f_far(k).wait_send()
        f_near(k).wait_send()
        f_cross(k).wait_send()
        g_near(k).wait_send()
        g_cross(k1).wait_send()
    for off in range(1, nm):
        basis_copy(off).wait_send()
        k_copy(off).wait_send()


def fused(mesh, velocity, radiation_modes, resistance, mode_ranks, freq_table):
    nb, nm = mesh.shape["band"], mesh.shape["mode"]
    patches, steps = velocity.shape[1:]
    mode_cols = radiation_modes.shape[1]
    modes = nm * mode_cols
    cols = 2 * (freq_table.shape[0] // nb)
    bf16, f32 = jnp.bfloat16, jnp.float32
    dma = lambda n: pltpu.SemaphoreType.DMA((n,))
    vmem = pl.BlockSpec(memory_space=pltpu.VMEM)
    out = pl.pallas_call(
        functools.partial(fused_kernel, nb, nm),
        out_shape=jax.ShapeDtypeStruct((patches, steps), bf16),
        in_specs=[vmem] * 5,
        out_specs=vmem,
        scratch_shapes=[
            pltpu.VMEM((nb, steps, cols), bf16),
            pltpu.VMEM((2, steps // HALF_ROWS, cols), f32),
            pltpu.VMEM((mode_cols, nm * patches), bf16),
            pltpu.VMEM((mode_cols, modes), bf16),
            pltpu.VMEM((mode_cols, modes), bf16),
            pltpu.VMEM((nb, nm, patches, cols), bf16),
            pltpu.VMEM((nb, mode_cols, cols), bf16),
            pltpu.VMEM((nb, mode_cols, cols), bf16),
            pltpu.VMEM((nm, mode_cols, cols), bf16),
            pltpu.VMEM((nb, nm, mode_cols, cols), bf16),
            pltpu.VMEM((nm, patches, mode_cols), bf16),
            pltpu.VMEM((patches, steps), f32),
            ]
        + [dma(nb) for _ in range(8)]
        + [dma(nm) for _ in range(4)]
        + [dma(nb) for _ in range(14)],
        compiler_params=pltpu.CompilerParams(collective_id=0, has_side_effects=True),
    )(velocity[0], radiation_modes, resistance[0], mode_ranks.reshape(1, 1), freq_table.reshape(nb // 2, cols))
    return out[None]


def make_table(freq_table, step_count):
    times = jnp.arange(step_count, dtype=jnp.int32)
    phases = times[:, None] * freq_table[None, :] % step_count
    angles = phases.astype(jnp.float32) * (2.0 * math.pi / step_count)
    norming = 1.0 / math.sqrt(step_count)
    table = jnp.stack([jnp.cos(angles), -jnp.sin(angles)], axis=1) * norming
    return table.astype(jnp.bfloat16)


def add_sources(received):
    return jnp.sum(received, axis=0)


def per_device(velocity, radiation_modes, resistance, mode_ranks, freq_table):
    step_count = velocity.shape[2]
    mode_cols = radiation_modes.shape[1]
    dft_table = make_table(freq_table, step_count)
    spectra = jnp.einsum(
        "wpt,tcf->wpcf", velocity, dft_table, preferred_element_type=jnp.float32
    ).astype(jnp.bfloat16)
    partial_value = jnp.einsum(
        "wpcf,pr->wrcf",
        lax.all_gather(spectra, "mode", axis=1, tiled=True),
        radiation_modes,
        preferred_element_type=jnp.float32,
    )
    coefficients = add_sources(
        lax.all_to_all(
            partial_value[None].astype(jnp.bfloat16),
            "band",
            split_axis=4,
            concat_axis=0,
            tiled=True,
        ).astype(jnp.float32)
    )
    offset = lax.axis_index("mode") * mode_cols
    rank_here = mode_ranks[0]
    kept_mask = (offset + jnp.arange(mode_cols, dtype=jnp.int32) < rank_here).astype(jnp.float32)
    kept_mask = kept_mask[None, :, None, None]
    coefficients = coefficients * kept_mask
    matrix = resistance[0]
    partial_terms = jnp.einsum(
        "ij,wjcf->wicf", matrix, coefficients, precision=lax.Precision.HIGHEST
    )
    forcing = lax.psum_scatter(
        partial_terms.astype(jnp.bfloat16), "mode", scatter_dimension=1, tiled=True
    ).astype(jnp.float32)
    forcing = (2.0 * forcing * kept_mask).astype(jnp.bfloat16)
    collected = lax.all_gather(forcing, "mode", axis=1, tiled=True)
    collected = lax.all_gather(collected, "band", axis=3, tiled=True)
    own_basis = lax.all_to_all(radiation_modes, "mode", split_axis=0, concat_axis=1, tiled=True)
    surface_force = jnp.einsum(
        "pr,wrcf->wpcf", own_basis, collected, preferred_element_type=jnp.float32
    ).astype(jnp.bfloat16)
    history = jnp.einsum(
        "wpcf,tcf->wpt", surface_force, dft_table, preferred_element_type=jnp.float32
    )
    return history.astype(jnp.bfloat16)


def solution(mesh):
    placed = (
        P(None, ("band", "mode"), None),
        P("band", "mode"),
        P("band", None, "mode"),
        P("band"),
        P(),
    )
    nb, nm = mesh.shape["band"], mesh.shape["mode"]

    def body(velocity, radiation_modes, resistance, mode_ranks, freq_table):
        windows, patches, steps = velocity.shape
        mode_cols = radiation_modes.shape[1]
        cols = 2 * (freq_table.shape[0] // nb)
        tiled = (
            windows == 1 and nm == 4 and nb == 8 and cols == 128 and mode_cols % 128 == 0
            and patches % 128 == 0 and steps % 128 == 0 and steps & (steps - 1) == 0
        )
        args = (velocity, radiation_modes, resistance, mode_ranks, freq_table)
        return fused(mesh, *args) if tiled else per_device(*args)

    return jax.shard_map(
        body,
        mesh=mesh,
        in_specs=placed,
        out_specs=P(None, ("band", "mode"), None),
        check_vma=False,
    )
```
